32 devices in a mesh: dp: 32 (over z, y, x, core).
Axes of the slice: x: 2, y: 2, z: 4, core: 2. Of those that a mesh axis runs over, the one named last changes fastest.
Arguments:
- events: bfloat16 [32768, 512], P('dp'), may hold values from -6 to 6
- home_slot: int32 [32768], P('dp'), may hold values from 0 to 1024, as said below
- dest_slot: int32 [32768], P('dp'), may hold values from 0 to 1024, as said below
- seq_lens: int32 [64], P('dp'), may hold values from 0 to 1024, as said below
- weights: bfloat16 [512, 2560], replicated, may hold values from -0.25 to 0.25
- out_grad: bfloat16 [32768, 512], P('dp'), may hold values from -6 to 6
- momentum_in: float32 [512, 2048], P('dp'), may hold values from -3 to 3
- momentum_out: float32 [512, 512], P('dp'), may hold values from -3 to 3
Outputs:
- event_grad: bfloat16 [32768, 512], P('dp')
- new_momentum_in: float32 [512, 2048], P('dp')
- new_momentum_out: float32 [512, 512], P('dp')
The draws below stay inside these ranges and needn't reach their ends.
Inputs may be any that keep to these rules, and one draw needn't show every extreme that they name: `seq_lens`: each device's 2 entries are the lengths of the sequences placed on it, in order, then zeros; the sequences' blocks, ceil(length / 512) each, add up to at most 2. `dest_slot`: for each row of a device's blocks: 1024 if the row lies in no sequence, else s * 32 + k, where s is the device that holds the row's event at home and k its slot among the rows that s sends to this device; no value below 1024 repeats on a device. `home_slot`: for each home row: 1024 if no sequence uses it, else t * 32 + k, where t is the device that takes the row and k its slot as in dest_slot; no value below 1024 repeats on a device, and the two arrays name the same rows. A device sends at most 32 rows to one device, and in every draw some device receives 32 rows from every device.
All inputs are finite; a program needn't handle non-finite values.
Results may differ from the reference program's by a relative error of at most 0.0085.
Values may be sent and summed in bfloat16 or wider, within the bound.
A program may use at most 128 MiB of HBM per device.

```python
import jax
import jax.numpy as jnp
from jax import lax

D = 512
HEADS = 8
BLK = 512
NBLK = 2
DEV_ROWS = 1024
ROWS = 32768


def row_owner_drawn(lengths, row_count):
    blocks = (lengths + BLK - 1) // BLK
    starts = (jnp.cumsum(blocks) - blocks) * BLK
    places = jnp.arange(row_count, dtype=jnp.int32)
    inside = (places[:, None] >= starts[None, :]) & (places[:, None] < starts[None, :] + lengths[None, :])
    labels = jnp.arange(lengths.shape[0], dtype=jnp.int32) + 1
    return (jnp.sum(jnp.where(inside, labels[None, :], 0), axis=1) - 1).astype(jnp.int32)


def placement_plan(base_key):
    devices = ROWS // DEV_ROWS
    capacity = DEV_ROWS // devices
    subkeys = jax.random.split(jax.random.fold_in(base_key, 7177), 6)
    device_ids = jnp.arange(devices, dtype=jnp.int32)
    block_ids = jnp.arange(NBLK, dtype=jnp.int32)
    used_blocks = jax.random.randint(subkeys[0], (devices,), (NBLK + 1) // 2, NBLK + 1, dtype=jnp.int32)
    crowded = jax.random.randint(subkeys[1], (), 0, devices, dtype=jnp.int32)
    used_blocks = jnp.where(device_ids == crowded, NBLK, used_blocks)
    breaks = jax.random.randint(subkeys[2], (devices, NBLK), 0, 2, dtype=jnp.int32)
    in_use = block_ids[None, :] < used_blocks[:, None]
    begins = jnp.where(block_ids[None, :] == 0, 1, breaks) * in_use.astype(jnp.int32)
    sequence_ids = (jnp.cumsum(begins, axis=1) - 1).astype(jnp.int32)
    matches = (sequence_ids[:, :, None] == block_ids[None, None, :]) & in_use[:, :, None]
    counts = jnp.sum(matches.astype(jnp.int32), axis=1).astype(jnp.int32)
    tail_rows = jax.random.randint(subkeys[3], (devices, NBLK), 1, BLK + 1, dtype=jnp.int32)
    tail_rows = jnp.where((device_ids == crowded)[:, None], BLK, tail_rows)
    lengths = jnp.where(counts > 0, (counts - 1) * BLK + tail_rows, 0).astype(jnp.int32)
    owners = jax.vmap(lambda entry: row_owner_drawn(entry, DEV_ROWS))(lengths)
    live_rows = (owners >= 0).astype(jnp.int32)
    rank_order = (jnp.cumsum(live_rows, axis=1) - 1).astype(jnp.int32)
    groups = jnp.clip(rank_order // capacity, 0, devices - 1)
    within = rank_order % capacity
    offsets = jax.random.permutation(subkeys[4], devices).astype(jnp.int32)
    sources = (device_ids[:, None] + offsets[groups]) % devices
    dest_slot = jnp.where(live_rows > 0, sources * capacity + within, DEV_ROWS).astype(jnp.int32)
    totals = jnp.sum(live_rows, axis=1).astype(jnp.int32)
    places = jnp.arange(DEV_ROWS, dtype=jnp.int32)
    place_group = places // capacity
    place_within = places % capacity
    targets = (device_ids[:, None] - offsets[place_group][None, :]) % devices
    values = jnp.where(places[None, :] < totals[targets], targets * capacity + place_within[None, :], DEV_ROWS).astype(jnp.int32)
    orders = jax.vmap(lambda subkey: jax.random.permutation(subkey, DEV_ROWS))(jax.random.split(subkeys[5], devices)).astype(jnp.int32)
    home_slot = jnp.zeros((devices, DEV_ROWS), jnp.int32).at[device_ids[:, None], orders].set(values)
    return (lengths, home_slot, dest_slot)


def draw_seq_lens(key, part):
    return placement_plan(key)[0].reshape(-1)


def draw_home_slot(key, part):
    return placement_plan(key)[1].reshape(-1)


def draw_dest_slot(key, part):
    return placement_plan(key)[2].reshape(-1)


def steps_of(rng, extent, cuts, smallest, largest):
    def one(dim, shards_of):
        steps = jax.random.uniform(jax.random.fold_in(jax.random.fold_in(rng, 6), dim), (shards_of,), jnp.float32, smallest / len(cuts), largest / len(cuts))
        return jnp.repeat(jnp.exp(steps), extent[dim] // shards_of).reshape((-1,) + (1,) * (len(extent) - dim - 1))

    level = one(*cuts[0])
    for cut in cuts[1:]:
        level = level * one(*cut)
    return level


def bell_draw(stream_key, dims, scale, most, cuts=(), kind=jnp.bfloat16):
    array = jax.random.normal(stream_key, dims, jnp.float32) * scale
    if len(cuts) > 0:
        array = steps_of(stream_key, dims, cuts, -0.22, 0.18) * array
    return jnp.clip(array, min=-most, max=most).astype(kind)


def setup_inputs(seed: int = 0) -> dict:
    streams_of = jax.random.split(jax.random.key(seed), 9)
    events = bell_draw(streams_of[0], (ROWS, D), 1.0, 6.0, ((0, 32),))
    home_slot = draw_home_slot(jax.random.fold_in(streams_of[8], 71), 0)
    dest_slot = draw_dest_slot(jax.random.fold_in(streams_of[8], 71), 0)
    seq_lens = draw_seq_lens(jax.random.fold_in(streams_of[8], 71), 0)
    weights = bell_draw(streams_of[4], (D, 5 * D), D ** -0.5, 0.25)
    out_grad = bell_draw(streams_of[5], (ROWS, D), 1.0, 6.0, ((0, 32),))
    momentum_in = bell_draw(streams_of[6], (D, 4 * D), 0.5, 3.0, ((0, 32),), jnp.float32)
    momentum_out = bell_draw(streams_of[7], (D, D), 0.5, 3.0, ((0, 32),), jnp.float32)
    return {"events": events, "home_slot": home_slot, "dest_slot": dest_slot, "seq_lens": seq_lens, "weights": weights, "out_grad": out_grad, "momentum_in": momentum_in, "momentum_out": momentum_out}


NORM_EPS = 1e-05
DECAY = 0.9

def row_owner(lengths, row_count):
    blocks = (lengths + BLK - 1) // BLK
    starts = (jnp.cumsum(blocks) - blocks) * BLK
    places = jnp.arange(row_count, dtype=jnp.int32)
    inside = (places[:, None] >= starts[None, :]) & (places[:, None] < starts[None, :] + lengths[None, :])
    labels = jnp.arange(lengths.shape[0], dtype=jnp.int32) + 1
    return (lax.optimization_barrier(jnp.sum(jnp.where(inside, labels[None, :], 0), axis=1)) - 1).astype(jnp.int32)

def attend_pair(queries, key_rows, value_rows, query_owner, key_owner, query_place, key_place):
    factor = queries.shape[2] ** (-0.5)
    scores = jnp.einsum('qhe,khe->hqk', queries.astype(jnp.float32), key_rows.astype(jnp.float32)) * factor
    allowed = (query_owner[:, None] == key_owner[None, :]) & (query_owner[:, None] >= 0) & (key_place[None, :] <= query_place[:, None])
    weights = jnp.where(allowed[None], jax.nn.silu(scores), 0.0).astype(jnp.bfloat16)
    return jnp.einsum('hqk,khe->qhe', weights.astype(jnp.float32), value_rows.astype(jnp.float32))

def mixing(hidden, owners):
    activated = jax.nn.silu(hidden)
    model_width = hidden.shape[1] // 4
    row_count = hidden.shape[0]
    head_size = model_width // HEADS
    gate_part = activated[:, :model_width]
    value_set = activated[:, model_width:2 * model_width].astype(jnp.bfloat16).reshape(row_count, HEADS, head_size)
    query_set = activated[:, 2 * model_width:3 * model_width].astype(jnp.bfloat16).reshape(row_count, HEADS, head_size)
    key_set = activated[:, 3 * model_width:].astype(jnp.bfloat16).reshape(row_count, HEADS, head_size)
    places = jnp.arange(row_count, dtype=jnp.int32)
    pieces = []
    for qblock in range(row_count // BLK):
        low_row = qblock * BLK
        high_row = low_row + BLK
        pieces.append(jax.checkpoint(attend_pair)(query_set[low_row:high_row], key_set[:high_row], value_set[:high_row], owners[low_row:high_row], owners[:high_row], places[low_row:high_row], places[:high_row]))
    attended = jnp.concatenate(pieces, axis=0).reshape(row_count, model_width)
    centre = lax.optimization_barrier(jnp.mean(attended, axis=1, keepdims=True))
    centred = attended - centre
    spread = lax.optimization_barrier(jnp.mean(centred * centred, axis=1, keepdims=True))
    return centred * lax.rsqrt(spread + NORM_EPS) * gate_part

def device_grads(tokens, upstream, weights, lengths):
    model_width = tokens.shape[1]
    owners = row_owner(lengths, tokens.shape[0])
    w_in = weights[:, :4 * model_width]
    w_out = weights[:, 4 * model_width:]
    hidden = jnp.dot(tokens, w_in, preferred_element_type=jnp.float32)
    mixed_out, pullback = jax.vjp(lambda hidden_in: mixing(hidden_in, owners), hidden)
    mixed_low = mixed_out.astype(jnp.bfloat16)
    mixed_grad = jnp.dot(upstream, w_out.T, preferred_element_type=jnp.float32)
    hidden_grad = pullback(mixed_grad)[0].astype(jnp.bfloat16)
    token_grad = (upstream.astype(jnp.float32) + jnp.dot(hidden_grad, w_in.T, preferred_element_type=jnp.float32)).astype(jnp.bfloat16)
    in_term = jnp.dot(tokens.T, hidden_grad, preferred_element_type=jnp.float32)
    out_term = jnp.dot(mixed_low.T, upstream, preferred_element_type=jnp.float32)
    return (token_grad, in_term, out_term)

def reference(events, home_slot, dest_slot, seq_lens, weights, out_grad, momentum_in, momentum_out):
    devices = ROWS // DEV_ROWS
    capacity = DEV_ROWS // devices
    model_width = events.shape[1]
    row_ids = jnp.arange(ROWS, dtype=jnp.int32)
    device_of = (row_ids // DEV_ROWS).astype(jnp.int32)
    send_keys = jnp.where(home_slot < DEV_ROWS, device_of * DEV_ROWS + home_slot, ROWS).astype(jnp.int32)
    lookup_table = jnp.full((ROWS + 1,), ROWS, dtype=jnp.int32).at[send_keys].set(row_ids)
    lookup_table = jnp.concatenate([lookup_table[:ROWS], jnp.full((1,), ROWS, dtype=jnp.int32)])
    receive_keys = jnp.where(dest_slot < DEV_ROWS, dest_slot // capacity * DEV_ROWS + device_of * capacity + dest_slot % capacity, ROWS).astype(jnp.int32)
    sources = lookup_table[receive_keys]
    padded = jnp.concatenate([events, jnp.zeros((1, model_width), jnp.bfloat16)], axis=0)
    tokens = padded[sources]

    def visit_device(running, entries):
        token_grad, in_term, out_term = device_grads(entries[0], entries[1], weights, entries[2])
        return ((running[0] + in_term, running[1] + out_term), token_grad)
    initial = (jnp.zeros((model_width, 4 * model_width), jnp.float32), jnp.zeros((model_width, model_width), jnp.float32))
    sums, token_grads = lax.scan(visit_device, initial, (tokens.reshape(devices, DEV_ROWS, model_width), out_grad.reshape(devices, DEV_ROWS, model_width), seq_lens.reshape(devices, NBLK)))
    event_grad = jnp.zeros((ROWS + 1, model_width), jnp.bfloat16).at[sources].set(token_grads.reshape(ROWS, model_width))[:ROWS]
    grad_scale = ROWS ** (-0.5)
    return (event_grad, DECAY * momentum_in + grad_scale * sums[0], DECAY * momentum_out + grad_scale * sums[1])
```

```python
import functools

import jax
import jax.numpy as jnp
from jax import lax
from jax.experimental import pallas as pl
from jax.experimental.pallas import tpu as pltpu
from jax.sharding import PartitionSpec as P

HEADS = 8
BLK = 512
QB = 256
NORM_EPS = 1e-05
DECAY = 0.9
MESH = pl.DeviceIdType.MESH
F32 = jnp.float32
BF16 = jnp.bfloat16
VMEM_LIMIT = 60 * 1024 * 1024


def dot_nn(a, b):
    return lax.dot_general(a, b, (((1,), (0,)), ((), ())), preferred_element_type=F32)


def dot_nt(a, b):
    return lax.dot_general(a, b, (((1,), (1,)), ((), ())), preferred_element_type=F32)


def dot_tn(a, b):
    return lax.dot_general(a, b, (((0,), (0,)), ((), ())), preferred_element_type=F32)


def chain_bits(bit_count, second):
    order = list(range(bit_count))
    if second and bit_count > 2:
        order[1], order[2] = order[2], order[1]
    return order


def enter_all(n, me):
    barrier = pltpu.get_barrier_semaphore()

    def greet(i, carry):
        pl.semaphore_signal(barrier, inc=1, device_id=((me + i) % n,), device_id_type=MESH)
        return carry

    lax.fori_loop(1, n, greet, 0)
    return barrier


def exchange(n, me, src, dst, ssem, rsem, i):
    peer = (me + i) % n
    return pltpu.make_async_remote_copy(
        src_ref=src.at[peer],
        dst_ref=dst.at[me],
        send_sem=ssem.at[i],
        recv_sem=rsem.at[i],
        device_id=(peer,),
        device_id_type=MESH,
    )


def start_exchange(n, me, src, dst, ssem, rsem):
    def go(i, carry):
        exchange(n, me, src, dst, ssem, rsem, i).start()
        return carry

    lax.fori_loop(n // 2, n, go, 0)
    lax.fori_loop(1, n // 2, go, 0)


def finish_exchange(n, me, src, dst, ssem, rsem):
    def end(i, carry):
        exchange(n, me, src, dst, ssem, rsem, i).wait()
        return carry

    lax.fori_loop(1, n, end, 0)


def gather_matrix(slots_ref, out_ref):
    rows = out_ref.shape[0]
    wide = jnp.broadcast_to(slots_ref[...].astype(F32), (128, rows))
    column = jnp.transpose(wide)
    lane = lax.broadcasted_iota(jnp.int32, (rows, 128), 1).astype(F32)
    for j in range(rows // 128):
        out_ref[:, j * 128 : (j + 1) * 128] = jnp.where(
            column == lane + float(j * 128), 1.0, 0.0
        ).astype(BF16)


def scatter_chunk(slots_ref, start, size):
    rows = slots_ref.shape[1]
    place = lax.broadcasted_iota(jnp.int32, (size, rows), 0) + start
    return jnp.where(place == slots_ref[...], 1.0, 0.0).astype(BF16)


def inbound_kernel(n, home_ref, dest_ref, ev_ref, tok_ref, outbox, inbox, pick, ssem, rsem):
    me = lax.axis_index("dp")
    rows, width = ev_ref.shape
    cap = rows // n
    barrier = enter_all(n, me)
    step = 256
    group = step // cap

    def fill(c, carry):
        part = dot_nn(scatter_chunk(home_ref, c * step, step), ev_ref[...]).astype(BF16)
        outbox[pl.ds(c * group, group)] = part.reshape(group, cap, width)
        return carry

    lax.fori_loop(0, rows // step, fill, 0)
    pl.semaphore_wait(barrier, n - 1)
    start_exchange(n, me, outbox, inbox, ssem, rsem)
    inbox[me] = outbox[me]
    gather_matrix(dest_ref, pick)
    finish_exchange(n, me, outbox, inbox, ssem, rsem)
    for c in range(rows // step):
        tok_ref[c * step : (c + 1) * step] = dot_nn(
            pick[c * step : (c + 1) * step], inbox[...].reshape(rows, width)
        ).astype(BF16)


def owner_of(place, lens_ref, none):
    owner = jnp.full(place.shape, none, jnp.int32)
    start = 0
    for j in range(lens_ref.shape[0]):
        length = lens_ref[j]
        inside = (place >= start) & (place < start + length)
        owner = jnp.where(inside, j, owner)
        start = start + (length + BLK - 1) // BLK * BLK
    return owner


def order_matrix(shape, n, per, bits):
    width = shape[1]
    place = lax.broadcasted_iota(jnp.int32, shape, 0)
    column = lax.broadcasted_iota(jnp.int32, shape, 1)
    slot = place // per
    device = jnp.zeros(shape, jnp.int32)
    for rank, bit in enumerate(bits):
        weight = n >> (rank + 1)
        device = device + ((slot // weight) % 2) * (1 << bit)
    return jnp.where(column == device * per + place % per, 1.0, 0.0).astype(BF16)


def layer_kernel(
    n, lens_ref, dest_ref, tok_ref, w_ref, og_ref,
    back_ref, ga_ref, gb_ref,
    slope, gate, qs, ks, vs, att, hgrad, mask, mask_t, mixed, dout, tgrad, acc_k, acc_v, tp,
):
    rows, width = tok_ref.shape
    per = width // n
    nq = rows // QB
    bits = n.bit_length() - 1

    def project(c, carry):
        r = pl.ds(pl.multiple_of(c * QB, QB), QB)
        x = tok_ref[r, :]
        for g in range(4):
            cols = slice(g * width, (g + 1) * width)
            u = dot_nn(x, w_ref[:, cols]) * 0.5
            t = jnp.tanh(u)
            a = u * t + u
            slope[r, cols] = 0.5 * ((1.0 + a) + t * (1.0 - a))
            if g == 0:
                gate[r, :] = a
            elif g == 1:
                vs[r, :] = a.astype(BF16)
            elif g == 2:
                qs[r, :] = (a.astype(BF16).astype(F32) * (0.5 * (width // HEADS) ** -0.5)).astype(BF16)
            else:
                ks[r, :] = a.astype(BF16)
        low = lax.broadcasted_iota(jnp.int32, (QB, rows), 0) + c * QB
        high = lax.broadcasted_iota(jnp.int32, (QB, rows), 1)
        low_col = lax.broadcasted_iota(jnp.int32, (QB, 1), 0) + c * QB
        high_row = lax.broadcasted_iota(jnp.int32, (1, rows), 1)
        q_own = owner_of(low_col, lens_ref, -1)
        k_own = owner_of(high_row, lens_ref, -2)
        mask[r, :] = jnp.where((q_own == k_own) & (high <= low), 1.0, 0.0).astype(BF16)
        mask_t[r, :] = jnp.where((q_own == k_own) & (low <= high), 1.0, 0.0).astype(BF16)
        return carry

    lax.fori_loop(0, nq, project, 0)

    pair_width = 128
    head = width // HEADS
    lane = lax.broadcasted_iota(jnp.int32, (1, pair_width), 1) // head
    picks = [jnp.where(lane == h, 1.0, 0.0).astype(BF16) for h in range(pair_width // head)]

    def forward(p, carry):
        cols = pl.ds(pl.multiple_of(p * pair_width, pair_width), pair_width)
        for c in range(nq):
            top = (c + 1) * QB
            r = slice(c * QB, top)
            out = None
            for sel in picks:
                u = dot_nt(qs[r, cols] * sel, ks[:top, cols])
                t = jnp.tanh(u)
                a = (u * t + u).astype(BF16) * mask[r, :top]
                o = dot_nn(a, vs[:top, cols] * sel)
                out = o if out is None else out + o
            att[r, cols] = out
        return carry

    lax.fori_loop(0, width // pair_width, forward, 0)

    def norm(c, carry):
        r = pl.ds(pl.multiple_of(c * QB, QB), QB)
        x = att[r, :]
        centred = x - jnp.mean(x, axis=1, keepdims=True)
        spread = jnp.mean(centred * centred, axis=1, keepdims=True)
        inv = lax.rsqrt(spread + NORM_EPS)
        unit = centred * inv
        g = gate[r, :]
        mixed[r, :] = (unit * g).astype(BF16)
        dmix = dot_nt(og_ref[r, :], w_ref[:, 4 * width :])
        hgrad[r, :width] = (dmix * unit * slope[r, :width]).astype(BF16)
        dn = dmix * g
        mean_a = jnp.mean(dn, axis=1, keepdims=True)
        mean_b = jnp.mean(dn * unit, axis=1, keepdims=True)
        dout[r, :] = (inv * (dn - mean_a - unit * mean_b)).astype(BF16)
        return carry

    lax.fori_loop(0, nq, norm, 0)

    def backward(p, carry):
        off = pl.multiple_of(p * pair_width, pair_width)
        cols = pl.ds(off, pair_width)
        for c in range(nq):
            top = (c + 1) * QB
            r = slice(c * QB, top)
            dq = None
            for sel in picks:
                qm = qs[r, cols] * sel
                dm = dout[r, cols] * sel
                u = dot_nt(ks[:top, cols], qm)
                t = jnp.tanh(u)
                a = u * t + u
                m = mask_t[:top, r]
                d = dot_nt(vs[:top, cols], dm)
                ds = (d * ((1.0 + a) + t * (1.0 - a))).astype(BF16) * m
                pb = a.astype(BF16) * m
                dv = dot_nn(pb, dm)
                dk = dot_nn(ds, qm)
                part = dot_tn(ds, ks[:top, cols] * sel)
                dq = part if dq is None else dq + part
                if c > 0:
                    acc_v[: c * QB, :] += dv[: c * QB]
                    acc_k[: c * QB, :] += dk[: c * QB]
                if sel is picks[0]:
                    acc_v[c * QB : top, :] = dv[c * QB :]
                    acc_k[c * QB : top, :] = dk[c * QB :]
                else:
                    acc_v[c * QB : top, :] += dv[c * QB :]
                    acc_k[c * QB : top, :] += dk[c * QB :]
            qcols = pl.ds(2 * width + off, pair_width)
            dq = (dq * (0.5 * head**-0.5)).astype(BF16).astype(F32)
            hgrad[r, qcols] = (dq * slope[r, qcols]).astype(BF16)
        vcols = pl.ds(width + off, pair_width)
        kcols = pl.ds(3 * width + off, pair_width)
        hgrad[:, vcols] = (acc_v[...].astype(BF16).astype(F32) * slope[:, vcols]).astype(BF16)
        hgrad[:, kcols] = (acc_k[...].astype(BF16).astype(F32) * slope[:, kcols]).astype(BF16)
        return carry

    lax.fori_loop(0, width // pair_width, backward, 0)

    def tokens_back(c, carry):
        r = pl.ds(pl.multiple_of(c * QB, QB), QB)
        tgrad[r, :] = (
            og_ref[r, :].astype(F32) + dot_nt(hgrad[r, :], w_ref[:, : 4 * width])
        ).astype(BF16)
        return carry

    lax.fori_loop(0, nq, tokens_back, 0)
    cap = rows // n
    group = QB // cap

    def send_rows(c, carry):
        part = dot_nn(scatter_chunk(dest_ref, c * QB, QB), tgrad[...]).astype(BF16)
        back_ref[pl.ds(c * group, group)] = part.reshape(group, cap, width)
        return carry

    lax.fori_loop(0, nq, send_rows, 0)

    half = ga_ref.shape[1]
    step = 256
    for ref, base, second in ((ga_ref, 0, False), (gb_ref, half, True)):
        order = order_matrix((width, width), n, per, chain_bits(bits, second))
        tp[...] = dot_nt(order, tok_ref[...]).astype(BF16)

        def columns(j, carry, ref=ref, base=base):
            src = pl.ds(pl.multiple_of(base + j * step, 128), step)
            dst = pl.ds(pl.multiple_of(j * step, 128), step)
            ref[:, dst] = dot_nn(tp[...], hgrad[:, src]).astype(BF16)
            return carry

        wide = min(half, 4 * width - base)
        lax.fori_loop(0, wide // step, columns, 0)
    tp[...] = dot_nt(order, mixed[...]).astype(BF16)
    gb_ref[:, wide:] = dot_nn(tp[...], og_ref[...]).astype(BF16)


def outbound_kernel(n, home_ref, back_ref, ga_ref, gb_ref, ev_ref, fa_ref, fb_ref, *scratch):
    bits = n.bit_length() - 1
    inbox, pick, ssem, rsem, hs, hr = scratch[:6]
    bufs = scratch[6:]
    me = lax.axis_index("dp")
    rows = pick.shape[0]
    width = inbox.shape[2]
    barrier = enter_all(n, me)
    pl.semaphore_wait(barrier, n - 1)

    def hop(chain, stage):
        bit = chain_bits(bits, chain == 1)[stage]
        mine = (me // (1 << bit)) % 2
        peer = me + (1 - 2 * mine) * (1 << bit)
        cur = (ga_ref, gb_ref)[chain] if stage == 0 else bufs[(chain * bits + stage - 1) * 2 + 1]
        got = bufs[(chain * bits + stage) * 2]
        half = cur.shape[0] // 2
        copy = pltpu.make_async_remote_copy(
            src_ref=cur.at[pl.ds((1 - mine) * half, half)],
            dst_ref=got,
            send_sem=hs.at[chain * bits + stage],
            recv_sem=hr.at[chain * bits + stage],
            device_id=(peer,),
            device_id_type=MESH,
        )
        return copy, cur.at[pl.ds(mine * half, half)], got

    live = [hop(0, 0), hop(1, 0)]
    for copy, _, _ in live:
        copy.start()
    start_exchange(n, me, back_ref, inbox, ssem, rsem)
    inbox[me] = back_ref[me]
    gather_matrix(home_ref, pick)
    for stage in range(bits):
        for chain in range(2):
            copy, kept, got = live[chain]
            copy.wait()
            total = kept[...].astype(F32) + got[...].astype(F32)
            if stage == bits - 1:
                (fa_ref, fb_ref)[chain][...] = total
            else:
                bufs[(chain * bits + stage) * 2 + 1][...] = total.astype(BF16)
                live[chain] = hop(chain, stage + 1)
                live[chain][0].start()
    finish_exchange(n, me, back_ref, inbox, ssem, rsem)
    step = 256
    for c in range(rows // step):
        ev_ref[c * step : (c + 1) * step] = dot_nn(
            pick[c * step : (c + 1) * step], inbox[...].reshape(rows, width)
        ).astype(BF16)


def shards(n, events, home_slot, dest_slot, seq_lens, weights, out_grad, momentum_in, momentum_out):
    rows, width = events.shape
    cap = rows // n
    bits = n.bit_length() - 1
    per = width // n
    home = home_slot.reshape(1, rows)
    dest = dest_slot.reshape(1, rows)
    vm = pl.BlockSpec(memory_space=pltpu.VMEM)
    sm = pl.BlockSpec(memory_space=pltpu.SMEM)
    dma = pltpu.SemaphoreType.DMA
    tokens = pl.pallas_call(
        functools.partial(inbound_kernel, n),
        out_shape=jax.ShapeDtypeStruct((rows, width), BF16),
        in_specs=[vm] * 3,
        out_specs=vm,
        scratch_shapes=[
            pltpu.VMEM((n, cap, width), BF16),
            pltpu.VMEM((n, cap, width), BF16),
            pltpu.VMEM((rows, rows), BF16),
            dma((n,)),
            dma((n,)),
        ],
        compiler_params=pltpu.CompilerParams(
            collective_id=0, has_side_effects=True, vmem_limit_bytes=VMEM_LIMIT
        ),
        name="inbound",
    )(home, dest, events)
    half = 5 * width // 2
    back, ga, gb = pl.pallas_call(
        functools.partial(layer_kernel, n),
        out_shape=[
            jax.ShapeDtypeStruct((n, cap, width), BF16),
            jax.ShapeDtypeStruct((width, half), BF16),
            jax.ShapeDtypeStruct((width, half), BF16),
        ],
        in_specs=[sm, vm, vm, vm, vm],
        out_specs=[vm] * 3,
        scratch_shapes=[
            pltpu.VMEM((rows, 4 * width), F32),
            pltpu.VMEM((rows, width), F32),
            pltpu.VMEM((rows, width), BF16),
            pltpu.VMEM((rows, width), BF16),
            pltpu.VMEM((rows, width), BF16),
            pltpu.VMEM((rows, width), F32),
            pltpu.VMEM((rows, 4 * width), BF16),
            pltpu.VMEM((rows, rows), BF16),
            pltpu.VMEM((rows, rows), BF16),
            pltpu.VMEM((rows, width), BF16),
            pltpu.VMEM((rows, width), BF16),
            pltpu.VMEM((rows, width), BF16),
            pltpu.VMEM((rows, 128), F32),
            pltpu.VMEM((rows, 128), F32),
            pltpu.VMEM((width, rows), BF16),
        ],
        compiler_params=pltpu.CompilerParams(vmem_limit_bytes=VMEM_LIMIT),
        name="layer",
    )(seq_lens, dest, tokens, weights, out_grad)
    tall = max(per, 16)
    thin = half * per // tall
    ga = ga.reshape(n * tall, thin)
    gb = gb.reshape(n * tall, thin)
    bufs = []
    for chain in range(2):
        for stage in range(bits):
            size = (n * tall >> (stage + 1), thin)
            bufs += [pltpu.VMEM(size, BF16), pltpu.VMEM(size, BF16)]
    event_grad, fa, fb = pl.pallas_call(
        functools.partial(outbound_kernel, n),
        out_shape=[
            jax.ShapeDtypeStruct((rows, width), BF16),
            jax.ShapeDtypeStruct((tall, thin), F32),
            jax.ShapeDtypeStruct((tall, thin), F32),
        ],
        in_specs=[vm] * 4,
        out_specs=[vm] * 3,
        scratch_shapes=[
            pltpu.VMEM((n, cap, width), BF16),
            pltpu.VMEM((rows, rows), BF16),
            dma((n,)),
            dma((n,)),
            dma((2 * bits,)),
            dma((2 * bits,)),
        ]
        + bufs,
        compiler_params=pltpu.CompilerParams(
            collective_id=1, has_side_effects=True, vmem_limit_bytes=VMEM_LIMIT
        ),
        name="outbound",
    )(home, back, ga, gb)
    sums = jnp.concatenate([fa.reshape(per, half), fb.reshape(per, half)], axis=1)
    grad_scale = (n * rows) ** (-0.5)
    return (
        event_grad,
        DECAY * momentum_in + grad_scale * sums[:, : 4 * width],
        DECAY * momentum_out + grad_scale * sums[:, 4 * width :],
    )


def solution(mesh):
    n = mesh.shape["dp"]
    row = P("dp", None)
    return jax.shard_map(
        functools.partial(shards, n),
        mesh=mesh,
        in_specs=(row, P("dp"), P("dp"), P("dp"), P(), row, row, row),
        out_specs=(row, row, row),
        check_vma=False,
    )
```

```python
import functools

import jax
import jax.numpy as jnp
from jax import lax
from jax.experimental import pallas as pl
from jax.experimental.pallas import tpu as pltpu
from jax.sharding import PartitionSpec as P

HEADS = 8
BLK = 512
QB = 256
NORM_EPS = 1e-05
DECAY = 0.9
MESH = pl.DeviceIdType.MESH
F32 = jnp.float32
BF16 = jnp.bfloat16
VMEM_LIMIT = 66 * 1000 * 1000


def dot_nn(a, b):
    return lax.dot_general(a, b, (((1,), (0,)), ((), ())), preferred_element_type=F32)


def dot_nt(a, b):
    return lax.dot_general(a, b, (((1,), (1,)), ((), ())), preferred_element_type=F32)


def dot_tn(a, b):
    return lax.dot_general(a, b, (((0,), (0,)), ((), ())), preferred_element_type=F32)


def chain_bits(bit_count, second):
    order = list(range(bit_count))
    if second and bit_count > 2:
        order[1], order[2] = order[2], order[1]
    return order


def enter_all(n, me):
    barrier = pltpu.get_barrier_semaphore()

    def greet(i, carry):
        pl.semaphore_signal(barrier, inc=1, device_id=((me + i) % n,), device_id_type=MESH)
        return carry

    lax.fori_loop(1, n, greet, 0)
    return barrier


def exchange(n, me, src, dst, ssem, rsem, i):
    peer = (me + i) % n
    return pltpu.make_async_remote_copy(
        src_ref=src.at[peer],
        dst_ref=dst.at[me],
        send_sem=ssem.at[i],
        recv_sem=rsem.at[i],
        device_id=(peer,),
        device_id_type=MESH,
    )


def start_exchange(n, me, src, dst, ssem, rsem):
    def go(i, carry):
        exchange(n, me, src, dst, ssem, rsem, i).start()
        return carry

    lax.fori_loop(n // 2, n, go, 0)
    lax.fori_loop(1, n // 2, go, 0)


def finish_exchange(n, me, src, dst, ssem, rsem):
    def end(i, carry):
        exchange(n, me, src, dst, ssem, rsem, i).wait()
        return carry

    lax.fori_loop(1, n, end, 0)


def gather_matrix(slots_ref, out_ref):
    rows = out_ref.shape[0]
    wide = jnp.broadcast_to(slots_ref[...].astype(F32), (128, rows))
    column = jnp.transpose(wide)
    lane = lax.broadcasted_iota(jnp.int32, (rows, 128), 1).astype(F32)
    for j in range(rows // 128):
        out_ref[:, j * 128 : (j + 1) * 128] = jnp.where(
            column == lane + float(j * 128), 1.0, 0.0
        ).astype(BF16)


def scatter_chunk(slots_ref, start, size):
    rows = slots_ref.shape[1]
    place = lax.broadcasted_iota(jnp.int32, (size, rows), 0) + start
    return jnp.where(place == slots_ref[...], 1.0, 0.0).astype(BF16)


def owner_of(place, lens_ref, none):
    owner = jnp.full(place.shape, none, jnp.int32)
    start = 0
    for j in range(lens_ref.shape[0]):
        length = lens_ref[j]
        inside = (place >= start) & (place < start + length)
        owner = jnp.where(inside, j, owner)
        start = start + (length + BLK - 1) // BLK * BLK
    return owner


def order_matrix(height, width, n, per, bits, fold, turn):
    shape = (height, width)
    tall = per * fold
    place = lax.broadcasted_iota(jnp.int32, shape, 0)
    column = lax.broadcasted_iota(jnp.int32, shape, 1)
    slot = place // tall
    rest = place % tall
    device = jnp.zeros(shape, jnp.int32)
    for rank, bit in enumerate(bits):
        weight = n >> (rank + 1)
        device = device + ((slot // weight) % 2) * (1 << bit)
    hit = (column == device * per + rest % per) & (rest // per == turn)
    return jnp.where(hit, 1.0, 0.0).astype(BF16)


def step_kernel(
    n, lens_ref, home_ref, dest_ref, ev_ref, w_hbm, og_hbm,
    ret_ref, f0_ref, f1_ref, f2_ref, f3_ref,
    w_ref, og_ref, outbox, inbox, inbox2, pick, tok_ref, dmix,
    slope, gate, qs, ks, vs, att, hgrad, mask, mask_t, mixed, dout, acc_k, acc_v, tp,
    lsem, ssem, rsem, ssem2, rsem2, hs, hr, *bufs,
):
    me = lax.axis_index("dp")
    rows, width = ev_ref.shape
    cap = rows // n
    per = width // n
    fold = max(1, 16 // per)
    nq = rows // QB
    bits = n.bit_length() - 1
    group = QB // cap
    barrier = enter_all(n, me)
    load_w = pltpu.make_async_copy(w_hbm, w_ref, lsem.at[0])
    load_og = pltpu.make_async_copy(og_hbm, og_ref, lsem.at[1])
    load_w.start()
    load_og.start()

    def fill(c, carry):
        part = dot_nn(scatter_chunk(home_ref, c * QB, QB), ev_ref[...]).astype(BF16)
        outbox[pl.ds(c * group, group)] = part.reshape(group, cap, width)
        return carry

    lax.fori_loop(0, nq, fill, 0)
    pl.semaphore_wait(barrier, n - 1)
    start_exchange(n, me, outbox, inbox, ssem, rsem)
    inbox[me] = outbox[me]
    gather_matrix(dest_ref, pick)
    load_w.wait()
    load_og.wait()

    def prepare(c, carry):
        r = pl.ds(pl.multiple_of(c * QB, QB), QB)
        low = lax.broadcasted_iota(jnp.int32, (QB, rows), 0) + c * QB
        high = lax.broadcasted_iota(jnp.int32, (QB, rows), 1)
        low_col = lax.broadcasted_iota(jnp.int32, (QB, 1), 0) + c * QB
        high_row = lax.broadcasted_iota(jnp.int32, (1, rows), 1)
        q_own = owner_of(low_col, lens_ref, -1)
        k_own = owner_of(high_row, lens_ref, -2)
        mask[r, :] = jnp.where((q_own == k_own) & (high <= low), 1.0, 0.0).astype(BF16)
        mask_t[r, :] = jnp.where((q_own == k_own) & (low <= high), 1.0, 0.0).astype(BF16)
        dmix[r, :] = dot_nt(og_ref[r, :], w_ref[:, 4 * width :]).astype(BF16)
        return carry

    lax.fori_loop(0, nq, prepare, 0)
    finish_exchange(n, me, outbox, inbox, ssem, rsem)

    def project(c, carry):
        r = pl.ds(pl.multiple_of(c * QB, QB), QB)
        x = dot_nn(pick[r, :], inbox[...].reshape(rows, width)).astype(BF16)
        tok_ref[r, :] = x
        for g in range(4):
            cols = slice(g * width, (g + 1) * width)
            u = dot_nn(x, w_ref[:, cols]) * 0.5
            t = jnp.tanh(u)
            a = u * t + u
            slope[r, cols] = (0.5 * ((1.0 + a) + t * (1.0 - a))).astype(BF16)
            if g == 0:
                gate[r, :] = a
            elif g == 1:
                vs[r, :] = a.astype(BF16)
            elif g == 2:
                qs[r, :] = (a.astype(BF16).astype(F32) * (0.5 * (width // HEADS) ** -0.5)).astype(BF16)
            else:
                ks[r, :] = a.astype(BF16)
        return carry

    lax.fori_loop(0, nq, project, 0)

    pair_width = 128
    head = width // HEADS
    lane = lax.broadcasted_iota(jnp.int32, (1, pair_width), 1) // head
    picks = [jnp.where(lane == h, 1.0, 0.0).astype(BF16) for h in range(pair_width // head)]

    def forward(p, carry):
        cols = pl.ds(pl.multiple_of(p * pair_width, pair_width), pair_width)
        for c in range(nq):
            top = (c + 1) * QB
            r = slice(c * QB, top)
            out = None
            for sel in picks:
                u = dot_nt(qs[r, cols] * sel, ks[:top, cols])
                t = jnp.tanh(u)
                a = (u * t + u).astype(BF16) * mask[r, :top]
                o = dot_nn(a, vs[:top, cols] * sel)
                out = o if out is None else out + o
            att[r, cols] = out
        return carry

    lax.fori_loop(0, width // pair_width, forward, 0)

    def norm(c, carry):
        r = pl.ds(pl.multiple_of(c * QB, QB), QB)
        x = att[r, :]
        centred = x - jnp.mean(x, axis=1, keepdims=True)
        spread = jnp.mean(centred * centred, axis=1, keepdims=True)
        inv = lax.rsqrt(spread + NORM_EPS)
        unit = centred * inv
        g = gate[r, :]
        mixed[r, :] = (unit * g).astype(BF16)
        dm = dmix[r, :].astype(F32)
        hgrad[r, :width] = (dm * unit * slope[r, :width]).astype(BF16)
        dn = dm * g
        mean_a = jnp.mean(dn, axis=1, keepdims=True)
        mean_b = jnp.mean(dn * unit, axis=1, keepdims=True)
        dout[r, :] = (inv * (dn - mean_a - unit * mean_b)).astype(BF16)
        return carry

    lax.fori_loop(0, nq, norm, 0)

    pairs = width // pair_width
    sources = bufs[:4]
    hops = bufs[4:]
    sums = (f0_ref, f1_ref, f2_ref, f3_ref)

    def hop(chain, stage):
        bit = chain_bits(bits, chain % 2 == 1)[stage]
        mine = (me // (1 << bit)) % 2
        peer = me + (1 - 2 * mine) * (1 << bit)
        cur = sources[chain] if stage == 0 else hops[chain * bits + stage - 1]
        got = hops[chain * bits + stage]
        half = cur.shape[0] // 2
        copy = pltpu.make_async_remote_copy(
            src_ref=cur.at[pl.ds((1 - mine) * half, half)],
            dst_ref=got,
            send_sem=hs.at[chain * bits + stage],
            recv_sem=hr.at[chain * bits + stage],
            device_id=(peer,),
            device_id_type=MESH,
        )
        return copy, cur.at[pl.ds(mine * half, half)], got

    def advance(chain, stage):
        copy, kept, got = hop(chain, stage)
        copy.wait()
        total = kept[...].astype(F32) + got[...].astype(F32)
        if stage == bits - 1:
            sums[chain][...] = total
        else:
            got[...] = total.astype(BF16)
            hop(chain, stage + 1)[0].start()

    def weight_grad(chain, left, right, base, wide):
        thin = wide // fold
        height = n * per * fold
        order = chain_bits(bits, chain % 2 == 1)
        for turn in range(fold):
            tp[...] = dot_nt(
                order_matrix(height, width, n, per, order, fold, turn), left[...]
            ).astype(BF16)
            step = 256 if thin % 256 == 0 else thin
            for j in range(thin // step):
                start = base + turn * thin + j * step
                part = dot_nn(tp[...], right[:, start : start + step])
                cols = slice(j * step, (j + 1) * step)
                if turn == 0:
                    sources[chain][:, cols] = part.astype(BF16)
                else:
                    sources[chain][:, cols] += part.astype(BF16)
        hop(chain, 0)[0].start()

    weight_grad(0, tok_ref, hgrad, 0, width)
    weight_grad(1, mixed, og_ref, 0, width)

    def backward(p, carry):
        off = pl.multiple_of(p * pair_width, pair_width)
        cols = pl.ds(off, pair_width)
        for c in range(nq):
            top = (c + 1) * QB
            r = slice(c * QB, top)
            dq = None
            for sel in picks:
                qm = qs[r, cols] * sel
                dm = dout[r, cols] * sel
                u = dot_nt(ks[:top, cols], qm)
                t = jnp.tanh(u)
                a = u * t + u
                m = mask_t[:top, r]
                d = dot_nt(vs[:top, cols], dm)
                ds = (d * ((1.0 + a) + t * (1.0 - a))).astype(BF16) * m
                pb = a.astype(BF16) * m
                dv = dot_nn(pb, dm)
                dk = dot_nn(ds, qm)
                part = dot_tn(ds, ks[:top, cols] * sel)
                dq = part if dq is None else dq + part
                if c > 0:
                    acc_v[: c * QB, :] += dv[: c * QB]
                    acc_k[: c * QB, :] += dk[: c * QB]
                if sel is picks[0]:
                    acc_v[c * QB : top, :] = dv[c * QB :]
                    acc_k[c * QB : top, :] = dk[c * QB :]
                else:
                    acc_v[c * QB : top, :] += dv[c * QB :]
                    acc_k[c * QB : top, :] += dk[c * QB :]
            qcols = pl.ds(2 * width + off, pair_width)
            dq = (dq * (0.5 * head**-0.5)).astype(BF16).astype(F32)
            hgrad[r, qcols] = (dq * slope[r, qcols]).astype(BF16)
        vcols = pl.ds(width + off, pair_width)
        kcols = pl.ds(3 * width + off, pair_width)
        hgrad[:, vcols] = (acc_v[...].astype(BF16).astype(F32) * slope[:, vcols]).astype(BF16)
        hgrad[:, kcols] = (acc_k[...].astype(BF16).astype(F32) * slope[:, kcols]).astype(BF16)
        for s in range(min(pairs, bits - 1)):

            @pl.when(p == s)
            def _():
                for chain in (0, 1):
                    advance(chain, s)

        return carry

    lax.fori_loop(0, pairs, backward, 0)

    def tokens_back(c, carry):
        r = pl.ds(pl.multiple_of(c * QB, QB), QB)
        dout[r, :] = (
            og_ref[r, :].astype(F32) + dot_nt(hgrad[r, :], w_ref[:, : 4 * width])
        ).astype(BF16)
        return carry

    lax.fori_loop(0, nq, tokens_back, 0)

    def send_rows(c, carry):
        part = dot_nn(scatter_chunk(dest_ref, c * QB, QB), dout[...]).astype(BF16)
        outbox[pl.ds(c * group, group)] = part.reshape(group, cap, width)
        return carry

    lax.fori_loop(0, nq, send_rows, 0)
    start_exchange(n, me, outbox, inbox2, ssem2, rsem2)
    wide = 3 * width // 2
    weight_grad(2, tok_ref, hgrad, width, wide)
    weight_grad(3, tok_ref, hgrad, width + wide, wide)
    inbox2[me] = outbox[me]
    for stage in range(min(pairs, bits - 1), bits):
        advance(0, stage)
        advance(1, stage)
    for stage in range(bits):
        advance(2, stage)
        advance(3, stage)
    finish_exchange(n, me, outbox, inbox2, ssem2, rsem2)
    store = pltpu.make_async_copy(inbox2, ret_ref, lsem.at[0])
    store.start()
    store.wait()


def finish_kernel(scale, home_ref, ret_ref, fi_ref, fo_ref, mi_ref, mo_ref, ev_ref, ni_ref, no_ref, pick):
    rows, width = ev_ref.shape
    gather_matrix(home_ref, pick)
    step = 256
    back = ret_ref[...].reshape(rows, width)
    for c in range(rows // step):
        ev_ref[c * step : (c + 1) * step] = dot_nn(pick[c * step : (c + 1) * step], back).astype(BF16)
    cols = 0
    for ref in fi_ref:
        wide = ref.shape[1]
        ni_ref[:, cols : cols + wide] = DECAY * mi_ref[:, cols : cols + wide] + scale * ref[...]
        cols += wide
    no_ref[...] = DECAY * mo_ref[...] + scale * fo_ref[...]


def finish_entry(scale, home, ret, fa, fb, fc, fo, mi, mo, ev, ni, no, pick):
    finish_kernel(scale, home, ret, (fa, fb, fc), fo, mi, mo, ev, ni, no, pick)


def shards(n, events, home_slot, dest_slot, seq_lens, weights, out_grad, momentum_in, momentum_out):
    rows, width = events.shape
    cap = rows // n
    bits = n.bit_length() - 1
    per = width // n
    fold = max(1, 16 // per)
    tall = per * fold
    home = home_slot.reshape(1, rows)
    dest = dest_slot.reshape(1, rows)
    vm = pl.BlockSpec(memory_space=pltpu.VMEM)
    sm = pl.BlockSpec(memory_space=pltpu.SMEM)
    hbm = pl.BlockSpec(memory_space=pl.ANY)
    dma = pltpu.SemaphoreType.DMA
    wides = (width, width, 3 * width // 2, 3 * width // 2)
    thins = [w // fold for w in wides]
    bufs = [pltpu.VMEM((n * tall, t), BF16) for t in thins]
    for t in thins:
        for stage in range(bits):
            size = (n * tall >> (stage + 1), t)
            bufs.append(pltpu.VMEM(size, BF16))

    def area(r, c, kind=BF16):
        return pltpu.VMEM((r, c), kind)

    boxed = pltpu.VMEM((n, cap, width), BF16)
    ret, *parts = pl.pallas_call(
        functools.partial(step_kernel, n),
        out_shape=[jax.ShapeDtypeStruct((n, cap, width), BF16)]
        + [jax.ShapeDtypeStruct((tall, t), F32) for t in thins],
        in_specs=[sm, vm, vm, vm, hbm, hbm],
        out_specs=[hbm] + [vm] * 4,
        scratch_shapes=[
            area(width, 5 * width),
            area(rows, width),
            boxed,
            boxed,
            boxed,
            area(rows, rows),
            area(rows, width),
            area(rows, width),
            area(rows, 4 * width),
            area(rows, width, F32),
            area(rows, width),
            area(rows, width),
            area(rows, width),
            area(rows, width, F32),
            area(rows, 4 * width),
            area(rows, rows),
            area(rows, rows),
            area(rows, width),
            area(rows, width),
            area(rows, 128, F32),
            area(rows, 128, F32),
            area(n * tall, rows),
            dma((2,)),
            dma((n,)),
            dma((n,)),
            dma((n,)),
            dma((n,)),
            dma((4 * bits,)),
            dma((4 * bits,)),
        ]
        + bufs,
        compiler_params=pltpu.CompilerParams(
            collective_id=0, has_side_effects=True, vmem_limit_bytes=VMEM_LIMIT
        ),
        name="step",
    )(seq_lens, home, dest, events, weights, out_grad)
    f0, f1, f2, f3 = [
        f.reshape(fold, per, f.shape[1]).transpose(1, 0, 2).reshape(per, fold * f.shape[1])
        for f in parts
    ]
    return pl.pallas_call(
        functools.partial(finish_entry, (n * rows) ** (-0.5)),
        out_shape=[
            jax.ShapeDtypeStruct(events.shape, BF16),
            jax.ShapeDtypeStruct(momentum_in.shape, F32),
            jax.ShapeDtypeStruct(momentum_out.shape, F32),
        ],
        in_specs=[vm] * 8,
        out_specs=[vm] * 3,
        scratch_shapes=[pltpu.VMEM((rows, rows), BF16)],
        compiler_params=pltpu.CompilerParams(vmem_limit_bytes=VMEM_LIMIT),
        name="finish",
    )(home, ret, f0, f2, f3, f1, momentum_in, momentum_out)


def solution(mesh):
    n = mesh.shape["dp"]
    row = P("dp", None)
    return jax.shard_map(
        functools.partial(shards, n),
        mesh=mesh,
        in_specs=(row, P("dp"), P("dp"), P("dp"), P(), row, row, row),
        out_specs=(row, row, row),
        check_vma=False,
    )
```

```python
import functools

import jax
import jax.numpy as jnp
from jax import lax
from jax.experimental import pallas as pl
from jax.experimental.pallas import tpu as pltpu
from jax.sharding import PartitionSpec as P

HEADS = 8
BLK = 512
QB = 256
SECOND = (False, True, False, True, False, False, True, True)
NORM_EPS = 1e-05
DECAY = 0.9
MESH = pl.DeviceIdType.MESH
F32 = jnp.float32
BF16 = jnp.bfloat16
VMEM_LIMIT = 66 * 1000 * 1000


def dot_nn(a, b):
    return lax.dot_general(a, b, (((1,), (0,)), ((), ())), preferred_element_type=F32)


def dot_nt(a, b):
    return lax.dot_general(a, b, (((1,), (1,)), ((), ())), preferred_element_type=F32)


def dot_tn(a, b):
    return lax.dot_general(a, b, (((0,), (0,)), ((), ())), preferred_element_type=F32)


def chain_bits(bit_count, second):
    order = list(range(bit_count))
    if second and bit_count > 2:
        order[1], order[2] = order[2], order[1]
    return order


def enter_all(n, me):
    barrier = pltpu.get_barrier_semaphore()

    def greet(i, carry):
        pl.semaphore_signal(barrier, inc=1, device_id=((me + i) % n,), device_id_type=MESH)
        return carry

    lax.fori_loop(1, n, greet, 0)
    return barrier


def exchange(n, me, src, dst, ssem, rsem, i):
    peer = (me + i) % n
    return pltpu.make_async_remote_copy(
        src_ref=src.at[peer],
        dst_ref=dst.at[me],
        send_sem=ssem.at[i],
        recv_sem=rsem.at[i],
        device_id=(peer,),
        device_id_type=MESH,
    )


def start_exchange(n, me, src, dst, ssem, rsem):
    def go(i, carry):
        exchange(n, me, src, dst, ssem, rsem, i).start()
        return carry

    lax.fori_loop(n // 2, n, go, 0)
    lax.fori_loop(1, n // 2, go, 0)


def finish_exchange(n, me, src, dst, ssem, rsem):
    def end(i, carry):
        exchange(n, me, src, dst, ssem, rsem, i).wait()
        return carry

    lax.fori_loop(1, n, end, 0)


def gather_matrix(slots_ref, out_ref):
    rows = out_ref.shape[0]
    wide = jnp.broadcast_to(slots_ref[...].astype(F32), (128, rows))
    column = jnp.transpose(wide)
    lane = lax.broadcasted_iota(jnp.int32, (rows, 128), 1).astype(F32)
    for j in range(rows // 128):
        out_ref[:, j * 128 : (j + 1) * 128] = jnp.where(
            column == lane + float(j * 128), 1.0, 0.0
        ).astype(BF16)


def scatter_chunk(slots_ref, start, size):
    rows = slots_ref.shape[1]
    place = lax.broadcasted_iota(jnp.int32, (size, rows), 0) + start
    return jnp.where(place == slots_ref[...], 1.0, 0.0).astype(BF16)


def owner_of(place, lens_ref, none):
    owner = jnp.full(place.shape, none, jnp.int32)
    start = 0
    for j in range(lens_ref.shape[0]):
        length = lens_ref[j]
        inside = (place >= start) & (place < start + length)
        owner = jnp.where(inside, j, owner)
        start = start + (length + BLK - 1) // BLK * BLK
    return owner


def order_matrix(height, width, n, per, bits, fold, turn):
    shape = (height, width)
    tall = per * fold
    place = lax.broadcasted_iota(jnp.int32, shape, 0)
    column = lax.broadcasted_iota(jnp.int32, shape, 1)
    slot = place // tall
    rest = place % tall
    device = jnp.zeros(shape, jnp.int32)
    for rank, bit in enumerate(bits):
        weight = n >> (rank + 1)
        device = device + ((slot // weight) % 2) * (1 << bit)
    hit = (column == device * per + rest % per) & (rest // per == turn)
    return jnp.where(hit, 1.0, 0.0).astype(BF16)


def step_kernel(
    n, lens_ref, home_ref, dest_ref, ev_ref, w_hbm, og_hbm,
    ret_ref, f0_ref, f1_ref, f2_ref, f3_ref, f4_ref, f5_ref, f6_ref, f7_ref,
    w_ref, og_ref, outbox, inbox, inbox2, pick, tok_ref, dmix,
    slope, gate, qs, ks, vs, att, hgrad, mask, mask_t, mixed, dout, acc_k, acc_v, tp,
    lsem, ssem, rsem, ssem2, rsem2, hs, hr, *bufs,
):
    me = lax.axis_index("dp")
    rows, width = ev_ref.shape
    cap = rows // n
    per = width // n
    fold = max(1, 16 // per)
    nq = rows // QB
    bits = n.bit_length() - 1
    group = QB // cap
    barrier = enter_all(n, me)
    load_w = pltpu.make_async_copy(w_hbm, w_ref, lsem.at[0])
    load_og = pltpu.make_async_copy(og_hbm, og_ref, lsem.at[1])
    load_w.start()
    load_og.start()

    def fill(c, carry):
        part = dot_nn(scatter_chunk(home_ref, c * QB, QB), ev_ref[...]).astype(BF16)
        outbox[pl.ds(c * group, group)] = part.reshape(group, cap, width)
        return carry

    lax.fori_loop(0, nq, fill, 0)
    pl.semaphore_wait(barrier, n - 1)
    start_exchange(n, me, outbox, inbox, ssem, rsem)
    inbox[me] = outbox[me]
    gather_matrix(dest_ref, pick)
    load_w.wait()
    load_og.wait()

    def prepare(c, carry):
        r = pl.ds(pl.multiple_of(c * QB, QB), QB)
        low = lax.broadcasted_iota(jnp.int32, (QB, rows), 0) + c * QB
        high = lax.broadcasted_iota(jnp.int32, (QB, rows), 1)
        low_col = lax.broadcasted_iota(jnp.int32, (QB, 1), 0) + c * QB
        high_row = lax.broadcasted_iota(jnp.int32, (1, rows), 1)
        q_own = owner_of(low_col, lens_ref, -1)
        k_own = owner_of(high_row, lens_ref, -2)
        mask[r, :] = jnp.where((q_own == k_own) & (high <= low), 1.0, 0.0).astype(BF16)
        mask_t[r, :] = jnp.where((q_own == k_own) & (low <= high), 1.0, 0.0).astype(BF16)
        dmix[r, :] = dot_nt(og_ref[r, :], w_ref[:, 4 * width :]).astype(BF16)
        return carry

    lax.fori_loop(0, nq, prepare, 0)
    finish_exchange(n, me, outbox, inbox, ssem, rsem)

    def project(c, carry):
        r = pl.ds(pl.multiple_of(c * QB, QB), QB)
        x = dot_nn(pick[r, :], inbox[...].reshape(rows, width)).astype(BF16)
        tok_ref[r, :] = x
        for g in range(4):
            cols = slice(g * width, (g + 1) * width)
            u = dot_nn(x, w_ref[:, cols]) * 0.5
            t = jnp.tanh(u)
            a = u * t + u
            slope[r, cols] = (0.5 * ((1.0 + a) + t * (1.0 - a))).astype(BF16)
            if g == 0:
                gate[r, :] = a
            elif g == 1:
                vs[r, :] = a.astype(BF16)
            elif g == 2:
                qs[r, :] = (a.astype(BF16).astype(F32) * (0.5 * (width // HEADS) ** -0.5)).astype(BF16)
            else:
                ks[r, :] = a.astype(BF16)
        return carry

    lax.fori_loop(0, nq, project, 0)

    pair_width = 128
    head = width // HEADS
    lane = lax.broadcasted_iota(jnp.int32, (1, pair_width), 1) // head
    picks = [jnp.where(lane == h, 1.0, 0.0).astype(BF16) for h in range(pair_width // head)]

    def forward(p, carry):
        cols = pl.ds(pl.multiple_of(p * pair_width, pair_width), pair_width)
        for c in range(nq):
            top = (c + 1) * QB
            r = slice(c * QB, top)
            out = None
            for sel in picks:
                u = dot_nt(qs[r, cols] * sel, ks[:top, cols])
                t = jnp.tanh(u)
                a = (u * t + u).astype(BF16) * mask[r, :top]
                o = dot_nn(a, vs[:top, cols] * sel)
                out = o if out is None else out + o
            att[r, cols] = out
        return carry

    lax.fori_loop(0, width // pair_width, forward, 0)

    def norm(c, carry):
        r = pl.ds(pl.multiple_of(c * QB, QB), QB)
        x = att[r, :]
        centred = x - jnp.mean(x, axis=1, keepdims=True)
        spread = jnp.mean(centred * centred, axis=1, keepdims=True)
        inv = lax.rsqrt(spread + NORM_EPS)
        unit = centred * inv
        g = gate[r, :]
        mixed[r, :] = (unit * g).astype(BF16)
        dm = dmix[r, :].astype(F32)
        hgrad[r, :width] = (dm * unit * slope[r, :width]).astype(BF16)
        dn = dm * g
        mean_a = jnp.mean(dn, axis=1, keepdims=True)
        mean_b = jnp.mean(dn * unit, axis=1, keepdims=True)
        dout[r, :] = (inv * (dn - mean_a - unit * mean_b)).astype(BF16)
        return carry

    lax.fori_loop(0, nq, norm, 0)

    pairs = width // pair_width
    sources = bufs[:8]
    hops = bufs[8:]
    sums = (f0_ref, f1_ref, f2_ref, f3_ref, f4_ref, f5_ref, f6_ref, f7_ref)

    def hop(chain, stage):
        bit = chain_bits(bits, SECOND[chain])[stage]
        mine = (me // (1 << bit)) % 2
        peer = me + (1 - 2 * mine) * (1 << bit)
        cur = sources[chain] if stage == 0 else hops[chain * bits + stage - 1]
        got = hops[chain * bits + stage]
        half = cur.shape[0] // 2
        copy = pltpu.make_async_remote_copy(
            src_ref=cur.at[pl.ds((1 - mine) * half, half)],
            dst_ref=got,
            send_sem=hs.at[chain * bits + stage],
            recv_sem=hr.at[chain * bits + stage],
            device_id=(peer,),
            device_id_type=MESH,
        )
        return copy, cur.at[pl.ds(mine * half, half)], got

    def advance(chain, stage):
        copy, kept, got = hop(chain, stage)
        copy.wait()
        total = kept[...].astype(F32) + got[...].astype(F32)
        if stage == bits - 1:
            sums[chain][...] = total
        else:
            got[...] = total.astype(BF16)
            hop(chain, stage + 1)[0].start()

    height = n * per * fold
    roomy = fold == 1 and 2 * height <= rows

    def turned(left, second, turn, out):
        order = order_matrix(height, width, n, per, chain_bits(bits, second), fold, turn)
        out[...] = dot_nt(order, left[...]).astype(BF16)
        return out

    if roomy:
        kept_rows = [
            turned(tok_ref, second, 0, pick.at[pl.ds(int(second) * height, height)])
            for second in (False, True)
        ]

    def weight_grad(chain, left, right, base, wide):
        thin = wide // fold
        for turn in range(fold):
            if roomy and left is tok_ref:
                lhs = kept_rows[int(SECOND[chain])]
            else:
                lhs = turned(left, SECOND[chain], turn, tp)
            step = 256 if thin % 256 == 0 else thin
            for j in range(thin // step):
                start = base + turn * thin + j * step
                part = dot_nn(lhs[...], right[:, start : start + step])
                cols = slice(j * step, (j + 1) * step)
                if turn == 0:
                    sources[chain][:, cols] = part.astype(BF16)
                else:
                    sources[chain][:, cols] += part.astype(BF16)
        hop(chain, 0)[0].start()

    def part_grads(second_half):
        for g in range(3):
            base = (g + 1) * width + second_half * (width // 2)
            weight_grad(2 + 3 * second_half + g, tok_ref, hgrad, base, width // 2)

    def advance_all(chains, stage):
        if stage < bits:
            for chain in chains:
                advance(chain, stage)

    weight_grad(0, tok_ref, hgrad, 0, width)
    weight_grad(1, mixed, og_ref, 0, width)

    def backward(p, carry):
        off = pl.multiple_of(p * pair_width, pair_width)
        cols = pl.ds(off, pair_width)
        for c in range(nq):
            top = (c + 1) * QB
            r = slice(c * QB, top)
            dq = None
            for sel in picks:
                qm = qs[r, cols] * sel
                dm = dout[r, cols] * sel
                u = dot_nt(ks[:top, cols], qm)
                t = jnp.tanh(u)
                a = u * t + u
                m = mask_t[:top, r]
                d = dot_nt(vs[:top, cols], dm)
                ds = (d * ((1.0 + a) + t * (1.0 - a))).astype(BF16) * m
                pb = a.astype(BF16) * m
                dv = dot_nn(pb, dm)
                dk = dot_nn(ds, qm)
                part = dot_tn(ds, ks[:top, cols] * sel)
                dq = part if dq is None else dq + part
                if c > 0:
                    acc_v[: c * QB, :] += dv[: c * QB]
                    acc_k[: c * QB, :] += dk[: c * QB]
                if sel is picks[0]:
                    acc_v[c * QB : top, :] = dv[c * QB :]
                    acc_k[c * QB : top, :] = dk[c * QB :]
                else:
                    acc_v[c * QB : top, :] += dv[c * QB :]
                    acc_k[c * QB : top, :] += dk[c * QB :]
            qcols = pl.ds(2 * width + off, pair_width)
            dq = (dq * (0.5 * head**-0.5)).astype(BF16).astype(F32)
            hgrad[r, qcols] = (dq * slope[r, qcols]).astype(BF16)
        vcols = pl.ds(width + off, pair_width)
        kcols = pl.ds(3 * width + off, pair_width)
        hgrad[:, vcols] = (acc_v[...].astype(BF16).astype(F32) * slope[:, vcols]).astype(BF16)
        hgrad[:, kcols] = (acc_k[...].astype(BF16).astype(F32) * slope[:, kcols]).astype(BF16)
        for s in range(pairs):

            @pl.when(p == s)
            def _():
                advance_all((0, 1), s)
                if s == pairs // 2 - 1:
                    part_grads(0)
                elif s >= pairs // 2:
                    advance_all((2, 3, 4), s - pairs // 2)

        return carry

    lax.fori_loop(0, pairs, backward, 0)
    part_grads(1)
    early = pairs - pairs // 2
    for stage in range(pairs, bits):
        advance_all((0, 1), stage)
    advance_all((2, 3, 4), early)

    def tokens_back(c, carry):
        r = pl.ds(pl.multiple_of(c * QB, QB), QB)
        dout[r, :] = (
            og_ref[r, :].astype(F32) + dot_nt(hgrad[r, :], w_ref[:, : 4 * width])
        ).astype(BF16)
        return carry

    lax.fori_loop(0, nq, tokens_back, 0)
    advance_all((2, 3, 4), early + 1)
    advance_all((5, 6, 7), 0)

    def send_rows(c, carry):
        part = dot_nn(scatter_chunk(dest_ref, c * QB, QB), dout[...]).astype(BF16)
        outbox[pl.ds(c * group, group)] = part.reshape(group, cap, width)
        return carry

    lax.fori_loop(0, nq, send_rows, 0)

    def some(low, high):
        def go(i, carry):
            exchange(n, me, outbox, inbox2, ssem2, rsem2, i).start()
            return carry

        lax.fori_loop(low, high, go, 0)

    some(n // 2, 7 * n // 8)
    inbox2[me] = outbox[me]
    for stage in range(early + 2, bits):
        advance_all((2, 3, 4), stage)
    advance_all((5, 6, 7), 1)
    some(7 * n // 8, n)
    some(1, n // 8)
    advance_all((5, 6, 7), 2)
    some(n // 8, n // 2)
    for stage in range(3, bits):
        advance_all((5, 6, 7), stage)
    finish_exchange(n, me, outbox, inbox2, ssem2, rsem2)
    store = pltpu.make_async_copy(inbox2, ret_ref, lsem.at[0])
    store.start()
    store.wait()


def finish_kernel(scale, home_ref, ret_ref, fi_ref, fo_ref, mi_ref, mo_ref, ev_ref, ni_ref, no_ref, pick):
    rows, width = ev_ref.shape
    gather_matrix(home_ref, pick)
    step = 256
    back = ret_ref[...].reshape(rows, width)
    for c in range(rows // step):
        ev_ref[c * step : (c + 1) * step] = dot_nn(pick[c * step : (c + 1) * step], back).astype(BF16)
    cols = 0
    for ref in fi_ref:
        wide = ref.shape[1]
        ni_ref[:, cols : cols + wide] = DECAY * mi_ref[:, cols : cols + wide] + scale * ref[...]
        cols += wide
    no_ref[...] = DECAY * mo_ref[...] + scale * fo_ref[...]


def finish_entry(scale, home, ret, f0, f1, f2, f3, f4, f5, f6, fo, mi, mo, ev, ni, no, pick):
    fi = (f0, f1, f2, f3, f4, f5, f6)
    finish_kernel(scale, home, ret, fi, fo, mi, mo, ev, ni, no, pick)


def shards(n, events, home_slot, dest_slot, seq_lens, weights, out_grad, momentum_in, momentum_out):
    rows, width = events.shape
    cap = rows // n
    bits = n.bit_length() - 1
    per = width // n
    fold = max(1, 16 // per)
    tall = per * fold
    home = home_slot.reshape(1, rows)
    dest = dest_slot.reshape(1, rows)
    vm = pl.BlockSpec(memory_space=pltpu.VMEM)
    sm = pl.BlockSpec(memory_space=pltpu.SMEM)
    hbm = pl.BlockSpec(memory_space=pl.ANY)
    dma = pltpu.SemaphoreType.DMA
    wides = (width, width) + (width // 2,) * 6
    thins = [w // fold for w in wides]
    bufs = [pltpu.VMEM((n * tall, t), BF16) for t in thins]
    for t in thins:
        for stage in range(bits):
            size = (n * tall >> (stage + 1), t)
            bufs.append(pltpu.VMEM(size, BF16))

    def area(r, c, kind=BF16):
        return pltpu.VMEM((r, c), kind)

    boxed = pltpu.VMEM((n, cap, width), BF16)
    ret, *parts = pl.pallas_call(
        functools.partial(step_kernel, n),
        out_shape=[jax.ShapeDtypeStruct((n, cap, width), BF16)]
        + [jax.ShapeDtypeStruct((tall, t), F32) for t in thins],
        in_specs=[sm, vm, vm, vm, hbm, hbm],
        out_specs=[hbm] + [vm] * 8,
        scratch_shapes=[
            area(width, 5 * width),
            area(rows, width),
            boxed,
            boxed,
            boxed,
            area(rows, rows),
            area(rows, width),
            area(rows, width),
            area(rows, 4 * width),
            area(rows, width, F32),
            area(rows, width),
            area(rows, width),
            area(rows, width),
            area(rows, width, F32),
            area(rows, 4 * width),
            area(rows, rows),
            area(rows, rows),
            area(rows, width),
            area(rows, width),
            area(rows, 128, F32),
            area(rows, 128, F32),
            area(n * tall, rows),
            dma((2,)),
            dma((n,)),
            dma((n,)),
            dma((n,)),
            dma((n,)),
            dma((8 * bits,)),
            dma((8 * bits,)),
        ]
        + bufs,
        compiler_params=pltpu.CompilerParams(
            collective_id=0, has_side_effects=True, vmem_limit_bytes=VMEM_LIMIT
        ),
        name="step",
    )(seq_lens, home, dest, events, weights, out_grad)
    gate_sum, out_sum, va, qa, ka, vb, qb, kb = [
        f.reshape(fold, per, f.shape[1]).transpose(1, 0, 2).reshape(per, fold * f.shape[1])
        for f in parts
    ]
    return pl.pallas_call(
        functools.partial(finish_entry, (n * rows) ** (-0.5)),
        out_shape=[
            jax.ShapeDtypeStruct(events.shape, BF16),
            jax.ShapeDtypeStruct(momentum_in.shape, F32),
            jax.ShapeDtypeStruct(momentum_out.shape, F32),
        ],
        in_specs=[vm] * 12,
        out_specs=[vm] * 3,
        scratch_shapes=[pltpu.VMEM((rows, rows), BF16)],
        compiler_params=pltpu.CompilerParams(vmem_limit_bytes=VMEM_LIMIT),
        name="finish",
    )(home, ret, gate_sum, va, vb, qa, qb, ka, kb, out_sum, momentum_in, momentum_out)


def inbound_kernel(n, home_ref, dest_ref, ev_ref, tok_ref, outbox, inbox, pick, ssem, rsem):
    me = lax.axis_index("dp")
    rows, width = ev_ref.shape
    cap = rows // n
    barrier = enter_all(n, me)
    step = 256
    group = step // cap

    def fill(c, carry):
        part = dot_nn(scatter_chunk(home_ref, c * step, step), ev_ref[...]).astype(BF16)
        outbox[pl.ds(c * group, group)] = part.reshape(group, cap, width)
        return carry

    lax.fori_loop(0, rows // step, fill, 0)
    pl.semaphore_wait(barrier, n - 1)
    start_exchange(n, me, outbox, inbox, ssem, rsem)
    inbox[me] = outbox[me]
    gather_matrix(dest_ref, pick)
    finish_exchange(n, me, outbox, inbox, ssem, rsem)
    for c in range(rows // step):
        tok_ref[c * step : (c + 1) * step] = dot_nn(
            pick[c * step : (c + 1) * step], inbox[...].reshape(rows, width)
        ).astype(BF16)


def order_plain(shape, n, per, bits):
    width = shape[1]
    place = lax.broadcasted_iota(jnp.int32, shape, 0)
    column = lax.broadcasted_iota(jnp.int32, shape, 1)
    slot = place // per
    device = jnp.zeros(shape, jnp.int32)
    for rank, bit in enumerate(bits):
        weight = n >> (rank + 1)
        device = device + ((slot // weight) % 2) * (1 << bit)
    return jnp.where(column == device * per + place % per, 1.0, 0.0).astype(BF16)


def layer_kernel(
    n, lens_ref, dest_ref, tok_ref, w_ref, og_ref,
    back_ref, ga_ref, gb_ref,
    slope, gate, qs, ks, vs, att, hgrad, mask, mask_t, mixed, dout, tgrad, acc_k, acc_v, tp,
):
    rows, width = tok_ref.shape
    per = width // n
    nq = rows // QB
    bits = n.bit_length() - 1

    def project(c, carry):
        r = pl.ds(pl.multiple_of(c * QB, QB), QB)
        x = tok_ref[r, :]
        for g in range(4):
            cols = slice(g * width, (g + 1) * width)
            u = dot_nn(x, w_ref[:, cols]) * 0.5
            t = jnp.tanh(u)
            a = u * t + u
            slope[r, cols] = 0.5 * ((1.0 + a) + t * (1.0 - a))
            if g == 0:
                gate[r, :] = a
            elif g == 1:
                vs[r, :] = a.astype(BF16)
            elif g == 2:
                qs[r, :] = (a.astype(BF16).astype(F32) * (0.5 * (width // HEADS) ** -0.5)).astype(BF16)
            else:
                ks[r, :] = a.astype(BF16)
        low = lax.broadcasted_iota(jnp.int32, (QB, rows), 0) + c * QB
        high = lax.broadcasted_iota(jnp.int32, (QB, rows), 1)
        low_col = lax.broadcasted_iota(jnp.int32, (QB, 1), 0) + c * QB
        high_row = lax.broadcasted_iota(jnp.int32, (1, rows), 1)
        q_own = owner_of(low_col, lens_ref, -1)
        k_own = owner_of(high_row, lens_ref, -2)
        mask[r, :] = jnp.where((q_own == k_own) & (high <= low), 1.0, 0.0).astype(BF16)
        mask_t[r, :] = jnp.where((q_own == k_own) & (low <= high), 1.0, 0.0).astype(BF16)
        return carry

    lax.fori_loop(0, nq, project, 0)

    pair_width = 128
    head = width // HEADS
    lane = lax.broadcasted_iota(jnp.int32, (1, pair_width), 1) // head
    picks = [jnp.where(lane == h, 1.0, 0.0).astype(BF16) for h in range(pair_width // head)]

    def forward(p, carry):
        cols = pl.ds(pl.multiple_of(p * pair_width, pair_width), pair_width)
        for c in range(nq):
            top = (c + 1) * QB
            r = slice(c * QB, top)
            out = None
            for sel in picks:
                u = dot_nt(qs[r, cols] * sel, ks[:top, cols])
                t = jnp.tanh(u)
                a = (u * t + u).astype(BF16) * mask[r, :top]
                o = dot_nn(a, vs[:top, cols] * sel)
                out = o if out is None else out + o
            att[r, cols] = out
        return carry

    lax.fori_loop(0, width // pair_width, forward, 0)

    def norm(c, carry):
        r = pl.ds(pl.multiple_of(c * QB, QB), QB)
        x = att[r, :]
        centred = x - jnp.mean(x, axis=1, keepdims=True)
        spread = jnp.mean(centred * centred, axis=1, keepdims=True)
        inv = lax.rsqrt(spread + NORM_EPS)
        unit = centred * inv
        g = gate[r, :]
        mixed[r, :] = (unit * g).astype(BF16)
        dmix = dot_nt(og_ref[r, :], w_ref[:, 4 * width :])
        hgrad[r, :width] = (dmix * unit * slope[r, :width]).astype(BF16)
        dn = dmix * g
        mean_a = jnp.mean(dn, axis=1, keepdims=True)
        mean_b = jnp.mean(dn * unit, axis=1, keepdims=True)
        dout[r, :] = (inv * (dn - mean_a - unit * mean_b)).astype(BF16)
        return carry

    lax.fori_loop(0, nq, norm, 0)

    def backward(p, carry):
        off = pl.multiple_of(p * pair_width, pair_width)
        cols = pl.ds(off, pair_width)
        for c in range(nq):
            top = (c + 1) * QB
            r = slice(c * QB, top)
            dq = None
            for sel in picks:
                qm = qs[r, cols] * sel
                dm = dout[r, cols] * sel
                u = dot_nt(ks[:top, cols], qm)
                t = jnp.tanh(u)
                a = u * t + u
                m = mask_t[:top, r]
                d = dot_nt(vs[:top, cols], dm)
                ds = (d * ((1.0 + a) + t * (1.0 - a))).astype(BF16) * m
                pb = a.astype(BF16) * m
                dv = dot_nn(pb, dm)
                dk = dot_nn(ds, qm)
                part = dot_tn(ds, ks[:top, cols] * sel)
                dq = part if dq is None else dq + part
                if c > 0:
                    acc_v[: c * QB, :] += dv[: c * QB]
                    acc_k[: c * QB, :] += dk[: c * QB]
                if sel is picks[0]:
                    acc_v[c * QB : top, :] = dv[c * QB :]
                    acc_k[c * QB : top, :] = dk[c * QB :]
                else:
                    acc_v[c * QB : top, :] += dv[c * QB :]
                    acc_k[c * QB : top, :] += dk[c * QB :]
            qcols = pl.ds(2 * width + off, pair_width)
            dq = (dq * (0.5 * head**-0.5)).astype(BF16).astype(F32)
            hgrad[r, qcols] = (dq * slope[r, qcols]).astype(BF16)
        vcols = pl.ds(width + off, pair_width)
        kcols = pl.ds(3 * width + off, pair_width)
        hgrad[:, vcols] = (acc_v[...].astype(BF16).astype(F32) * slope[:, vcols]).astype(BF16)
        hgrad[:, kcols] = (acc_k[...].astype(BF16).astype(F32) * slope[:, kcols]).astype(BF16)
        return carry

    lax.fori_loop(0, width // pair_width, backward, 0)

    def tokens_back(c, carry):
        r = pl.ds(pl.multiple_of(c * QB, QB), QB)
        tgrad[r, :] = (
            og_ref[r, :].astype(F32) + dot_nt(hgrad[r, :], w_ref[:, : 4 * width])
        ).astype(BF16)
        return carry

    lax.fori_loop(0, nq, tokens_back, 0)
    cap = rows // n
    group = QB // cap

    def send_rows(c, carry):
        part = dot_nn(scatter_chunk(dest_ref, c * QB, QB), tgrad[...]).astype(BF16)
        back_ref[pl.ds(c * group, group)] = part.reshape(group, cap, width)
        return carry

    lax.fori_loop(0, nq, send_rows, 0)

    half = ga_ref.shape[1]
    step = 256
    for ref, base, second in ((ga_ref, 0, False), (gb_ref, half, True)):
        order = order_plain((width, width), n, per, chain_bits(bits, second))
        tp[...] = dot_nt(order, tok_ref[...]).astype(BF16)

        def columns(j, carry, ref=ref, base=base):
            src = pl.ds(pl.multiple_of(base + j * step, 128), step)
            dst = pl.ds(pl.multiple_of(j * step, 128), step)
            ref[:, dst] = dot_nn(tp[...], hgrad[:, src]).astype(BF16)
            return carry

        wide = min(half, 4 * width - base)
        lax.fori_loop(0, wide // step, columns, 0)
    tp[...] = dot_nt(order, mixed[...]).astype(BF16)
    gb_ref[:, wide:] = dot_nn(tp[...], og_ref[...]).astype(BF16)


def outbound_kernel(n, home_ref, back_ref, ga_ref, gb_ref, ev_ref, fa_ref, fb_ref, *scratch):
    bits = n.bit_length() - 1
    inbox, pick, ssem, rsem, hs, hr = scratch[:6]
    bufs = scratch[6:]
    me = lax.axis_index("dp")
    rows = pick.shape[0]
    width = inbox.shape[2]
    barrier = enter_all(n, me)
    pl.semaphore_wait(barrier, n - 1)

    def hop(chain, stage):
        bit = chain_bits(bits, chain == 1)[stage]
        mine = (me // (1 << bit)) % 2
        peer = me + (1 - 2 * mine) * (1 << bit)
        cur = (ga_ref, gb_ref)[chain] if stage == 0 else bufs[(chain * bits + stage - 1) * 2 + 1]
        got = bufs[(chain * bits + stage) * 2]
        half = cur.shape[0] // 2
        copy = pltpu.make_async_remote_copy(
            src_ref=cur.at[pl.ds((1 - mine) * half, half)],
            dst_ref=got,
            send_sem=hs.at[chain * bits + stage],
            recv_sem=hr.at[chain * bits + stage],
            device_id=(peer,),
            device_id_type=MESH,
        )
        return copy, cur.at[pl.ds(mine * half, half)], got

    live = [hop(0, 0), hop(1, 0)]
    for copy, _, _ in live:
        copy.start()
    start_exchange(n, me, back_ref, inbox, ssem, rsem)
    inbox[me] = back_ref[me]
    gather_matrix(home_ref, pick)
    for stage in range(bits):
        for chain in range(2):
            copy, kept, got = live[chain]
            copy.wait()
            total = kept[...].astype(F32) + got[...].astype(F32)
            if stage == bits - 1:
                (fa_ref, fb_ref)[chain][...] = total
            else:
                bufs[(chain * bits + stage) * 2 + 1][...] = total.astype(BF16)
                live[chain] = hop(chain, stage + 1)
                live[chain][0].start()
    finish_exchange(n, me, back_ref, inbox, ssem, rsem)
    step = 256
    for c in range(rows // step):
        ev_ref[c * step : (c + 1) * step] = dot_nn(
            pick[c * step : (c + 1) * step], inbox[...].reshape(rows, width)
        ).astype(BF16)


def shards_small(n, events, home_slot, dest_slot, seq_lens, weights, out_grad, momentum_in, momentum_out):
    rows, width = events.shape
    cap = rows // n
    bits = n.bit_length() - 1
    per = width // n
    home = home_slot.reshape(1, rows)
    dest = dest_slot.reshape(1, rows)
    vm = pl.BlockSpec(memory_space=pltpu.VMEM)
    sm = pl.BlockSpec(memory_space=pltpu.SMEM)
    dma = pltpu.SemaphoreType.DMA
    tokens = pl.pallas_call(
        functools.partial(inbound_kernel, n),
        out_shape=jax.ShapeDtypeStruct((rows, width), BF16),
        in_specs=[vm] * 3,
        out_specs=vm,
        scratch_shapes=[
            pltpu.VMEM((n, cap, width), BF16),
            pltpu.VMEM((n, cap, width), BF16),
            pltpu.VMEM((rows, rows), BF16),
            dma((n,)),
            dma((n,)),
        ],
        compiler_params=pltpu.CompilerParams(
            collective_id=0, has_side_effects=True, vmem_limit_bytes=VMEM_LIMIT
        ),
        name="inbound",
    )(home, dest, events)
    half = 5 * width // 2
    back, ga, gb = pl.pallas_call(
        functools.partial(layer_kernel, n),
        out_shape=[
            jax.ShapeDtypeStruct((n, cap, width), BF16),
            jax.ShapeDtypeStruct((width, half), BF16),
            jax.ShapeDtypeStruct((width, half), BF16),
        ],
        in_specs=[sm, vm, vm, vm, vm],
        out_specs=[vm] * 3,
        scratch_shapes=[
            pltpu.VMEM((rows, 4 * width), F32),
            pltpu.VMEM((rows, width), F32),
            pltpu.VMEM((rows, width), BF16),
            pltpu.VMEM((rows, width), BF16),
            pltpu.VMEM((rows, width), BF16),
            pltpu.VMEM((rows, width), F32),
            pltpu.VMEM((rows, 4 * width), BF16),
            pltpu.VMEM((rows, rows), BF16),
            pltpu.VMEM((rows, rows), BF16),
            pltpu.VMEM((rows, width), BF16),
            pltpu.VMEM((rows, width), BF16),
            pltpu.VMEM((rows, width), BF16),
            pltpu.VMEM((rows, 128), F32),
            pltpu.VMEM((rows, 128), F32),
            pltpu.VMEM((width, rows), BF16),
        ],
        compiler_params=pltpu.CompilerParams(vmem_limit_bytes=VMEM_LIMIT),
        name="layer",
    )(seq_lens, dest, tokens, weights, out_grad)
    tall = max(per, 16)
    thin = half * per // tall
    ga = ga.reshape(n * tall, thin)
    gb = gb.reshape(n * tall, thin)
    bufs = []
    for chain in range(2):
        for stage in range(bits):
            size = (n * tall >> (stage + 1), thin)
            bufs += [pltpu.VMEM(size, BF16), pltpu.VMEM(size, BF16)]
    event_grad, fa, fb = pl.pallas_call(
        functools.partial(outbound_kernel, n),
        out_shape=[
            jax.ShapeDtypeStruct((rows, width), BF16),
            jax.ShapeDtypeStruct((tall, thin), F32),
            jax.ShapeDtypeStruct((tall, thin), F32),
        ],
        in_specs=[vm] * 4,
        out_specs=[vm] * 3,
        scratch_shapes=[
            pltpu.VMEM((n, cap, width), BF16),
            pltpu.VMEM((rows, rows), BF16),
            dma((n,)),
            dma((n,)),
            dma((2 * bits,)),
            dma((2 * bits,)),
        ]
        + bufs,
        compiler_params=pltpu.CompilerParams(
            collective_id=1, has_side_effects=True, vmem_limit_bytes=VMEM_LIMIT
        ),
        name="outbound",
    )(home, back, ga, gb)
    sums = jnp.concatenate([fa.reshape(per, half), fb.reshape(per, half)], axis=1)
    grad_scale = (n * rows) ** (-0.5)
    return (
        event_grad,
        DECAY * momentum_in + grad_scale * sums[:, : 4 * width],
        DECAY * momentum_out + grad_scale * sums[:, 4 * width :],
    )


def solution(mesh):
    n = mesh.shape["dp"]
    row = P("dp", None)
    return jax.shard_map(
        functools.partial(shards if BLK // n >= 16 else shards_small, n),
        mesh=mesh,
        in_specs=(row, P("dp"), P("dp"), P("dp"), P(), row, row, row),
        out_specs=(row, row, row),
        check_vma=False,
    )
```
